32 devices in a mesh: segment: 2 (over core), dp: 4 (over y, x), mp: 4 (over z).
Axes of the slice: x: 2, y: 2, z: 4, core: 2. Of those that a mesh axis runs over, the one named last changes fastest.
Arguments:
- queries: bfloat16 [2, 8, 256, 4096], P('segment', 'dp', None, 'mp'), may hold values from -500 to 500
- vision: bfloat16 [8, 48, 8192], P('dp', 'segment'), may hold values from -6 to 6
- w_key: bfloat16 [2, 8192, 512], P('segment', None, 'mp'), may hold values from -0.0625 to 0.0625
- w_value: bfloat16 [2, 8192, 512], P('segment', None, 'mp'), may hold values from -0.0625 to 0.0625
- masks: int32 [8, 2, 2], P('dp'), may hold values 0 or 1
- lengths: int32 [8], P('dp'), may hold values from 1 to 256, as said below
- grad_context: bfloat16 [2, 8, 256, 4096], P('segment', 'dp', None, 'mp'), may hold values from -6 to 6
Outputs:
- context: bfloat16 [2, 8, 256, 4096], P('segment', 'dp', None, 'mp')
- grad_vision: float32 [4, 96, 8192], P('dp', ('segment', 'mp'))
- grad_w_key: float32 [2, 8192, 512], P('segment', 'dp', 'mp')
- grad_w_value: float32 [2, 8192, 512], P('segment', 'dp', 'mp')
The draws below stay inside these ranges and needn't reach their ends.
Inputs may be any that keep to these rules, and one draw needn't show every extreme that they name: `lengths`: some sample has all 256 positions.
All inputs are finite; a program needn't handle non-finite values. No bound on the sum of `masks` on one device may be relied on, other than what follows from the above.
Results may differ from the reference program's by a relative error of at most 0.011.
Values may be sent and summed in bfloat16 or wider, within the bound.
No kernel may reach another device: no remote copies, remote signals or barrier semaphores. Data moves between devices by JAX's collectives and lax.ppermute only.
A program may use at most 64 MiB of HBM per device.

```python
import math
import jax
import jax.numpy as jnp
from jax import lax

D = 8192
HD = 128
HQ_DEV = 8
HEADS = 32
KV_HEADS = 4
LT = 256
TB = 128
TBLK = 2
MB = 2
MBS = 8
TILES = 2
TILE_TOK = 24
VT = 48
N_SEGMENT = 2
N_DP = 4


def draw_queries(key, part):
    row_key, column_key, base_key = jax.random.split(key, 3)
    full_shape = (N_SEGMENT, MBS, LT, HEADS * HD)
    row_scale = jnp.exp(jax.random.uniform(row_key, (N_SEGMENT, MBS, LT, 1), jnp.float32, 0.0, math.log(10.0)))
    column_scale = jnp.exp(jax.random.uniform(column_key, (1, 1, 1, HEADS * HD), jnp.float32, 0.0, math.log(10.0)))
    base = jax.random.normal(base_key, full_shape, jnp.float32)
    return jnp.clip(base * row_scale * column_scale, -500.0, 500.0).astype(jnp.bfloat16)


def draw_lengths(key, part):
    sampled = jax.random.randint(key, (MBS,), 1, LT + 1, dtype=jnp.int32)
    return sampled.at[0].set(LT)


def touch_ends(values, stream_key, smallest, high):
    index_at = [jax.random.randint(jax.random.fold_in(stream_key, axis), (), 0, length) for axis, length in enumerate(values.shape)]
    longest = values.shape.index(max(values.shape))
    beside = index_at[:longest] + [(index_at[longest] + 1) % values.shape[longest]] + index_at[longest + 1:]
    return values.at[tuple(index_at)].set(smallest).at[tuple(beside)].set(high)


def spiked(result, own_key, source, target, shards_of, factor):
    def block_of(dim):
        return (jnp.arange(result.shape[dim]) // (result.shape[dim] // shards_of)).reshape((-1,) + (1,) * (result.ndim - 1 - dim))

    one_side = jax.random.permutation(own_key, shards_of)[block_of(target)]
    far = (block_of(target) + shards_of // 2) % shards_of
    return jnp.where((block_of(source) == one_side) | (block_of(source) == far), factor * result, result)


def shard_levels(rng, shape, shards, low, top_value):
    factor_of, own = 1.0, jax.random.fold_in(rng, 6)
    for dim, blocks in shards:
        heights = jnp.exp(jax.random.uniform(jax.random.fold_in(own, dim), (blocks,), jnp.float32, low / len(shards), top_value / len(shards)))
        factor_of = factor_of * jnp.repeat(heights, shape[dim] // blocks).reshape([-1 if axis == dim else 1 for axis in range(len(shape))])
    return factor_of


def normal_values(own_key, shape, scale, reach, pieces=(), kind=jnp.bfloat16):
    gain = shard_levels(own_key, shape, pieces, -0.22, 0.18) if pieces else 1.0
    entries = jax.random.normal(own_key, shape, jnp.float32) * scale * gain
    return jnp.minimum(jnp.maximum(entries, -reach), reach).astype(kind)


def bell_draw_with(rng, shape, deviation, most, pieces, heavy, kind=jnp.bfloat16):
    drawn = deviation * jax.random.normal(rng, shape, jnp.float32)
    if pieces:
        drawn = drawn * shard_levels(rng, shape, pieces, -0.22, 0.18)
    return jnp.clip(spiked(drawn, jax.random.fold_in(rng, 3), *heavy), -most, most).astype(kind)


def setup_inputs(seed: int = 0) -> dict:
    key_of = jax.random.split(jax.random.key(seed), 8)
    queries = draw_queries(jax.random.fold_in(key_of[7], 71), 0)
    vision = bell_draw_with(key_of[1], (MBS, VT, D), 1.0, 6.0, ((0, 4), (1, 2)), (0, 2, 4, 2.0))
    w_key = normal_values(key_of[2], (N_SEGMENT, D, KV_HEADS * HD), D ** -0.5, 0.0625, ((0, 2), (2, 4)))
    w_value = normal_values(key_of[3], (N_SEGMENT, D, KV_HEADS * HD), D ** -0.5, 0.0625, ((0, 2), (2, 4)))
    masks = touch_ends((jax.random.randint(key_of[4], (MBS, TBLK, TILES), 0, 3) < 2).astype(jnp.int32), jax.random.fold_in(key_of[4], 1), 0, 1)
    lengths = draw_lengths(jax.random.fold_in(key_of[7], 71), 0)
    grad_context = normal_values(key_of[6], (N_SEGMENT, MBS, LT, HEADS * HD), 1.0, 6.0, ((0, 2), (1, 4), (3, 4)))
    return {"queries": queries, "vision": vision, "w_key": w_key, "w_value": w_value, "masks": masks, "lengths": lengths, "grad_context": grad_context}


EPSILON = 1e-06

def normalize(values_in):
    factor = lax.rsqrt(lax.optimization_barrier(jnp.mean(values_in * values_in, axis=-1, keepdims=True)) + EPSILON)
    return (values_in * factor, factor)

def reference(queries, vision, w_key, w_value, masks, lengths, grad_context):
    samples = vision.shape[0]
    tile_rows = vision.shape[1]
    groups = w_key.shape[2] // HD
    flat_rows = samples * tile_rows
    group_rows = MB * tile_rows
    root_scale = 1.0 / math.sqrt(HD)
    spread = jnp.broadcast_to(masks[:, :, None, :, None], (samples, LT // TB, TB, TILES, TILE_TOK)).reshape(samples, LT, tile_rows)
    position = jnp.arange(LT, dtype=jnp.int32)
    allowed = jnp.where((spread == 1) & (position[None, :, None] < lengths[:, None, None]), 1.0, 0.0).astype(jnp.float32)
    flat_vision = vision.reshape(flat_rows, D)
    contexts = []
    key_totals = []
    value_totals = []
    vision_grad = jnp.zeros((flat_rows, D), jnp.float32)
    for section in range(N_SEGMENT):
        key_raw = jnp.dot(flat_vision, w_key[section], preferred_element_type=jnp.float32).reshape(flat_rows, groups, HD)
        key_norm, key_factor = normalize(key_raw)
        key_rows = key_norm.astype(jnp.bfloat16).reshape(samples, tile_rows, groups, HD)
        value_rows = jnp.dot(flat_vision, w_value[section], preferred_element_type=jnp.float32).astype(jnp.bfloat16)
        value_rows = value_rows.reshape(samples, tile_rows, groups, HD)
        query_raw = queries[section].astype(jnp.float32).reshape(samples, LT, groups, HQ_DEV, HD)
        query_rows = normalize(query_raw)[0].astype(jnp.bfloat16)
        scores = jnp.einsum('btghd,bjgd->bghtj', query_rows.astype(jnp.float32), key_rows.astype(jnp.float32)) * root_scale
        exponent = jnp.exp(scores) * allowed[:, None, None]
        denominator = lax.optimization_barrier(jnp.sum(exponent, axis=-1, keepdims=True))
        probability = exponent / jnp.where(denominator > 0, denominator, 1.0)
        weights = probability.astype(jnp.bfloat16)
        context = jnp.einsum('bghtj,bjgd->btghd', weights.astype(jnp.float32), value_rows.astype(jnp.float32))
        contexts.append(context.astype(jnp.bfloat16).reshape(samples, LT, groups * HQ_DEV * HD))
        grad_rows = grad_context[section].astype(jnp.float32).reshape(samples, LT, groups, HQ_DEV, HD)
        grad_weights = jnp.einsum('btghd,bjgd->bghtj', grad_rows, value_rows.astype(jnp.float32))
        grad_scores = probability * (grad_weights - lax.optimization_barrier(jnp.sum(probability * grad_weights, axis=-1, keepdims=True))) * root_scale
        grad_scores = grad_scores.astype(jnp.bfloat16)
        grad_key_norm = jnp.einsum('bghtj,btghd->bjgd', grad_scores.astype(jnp.float32), query_rows.astype(jnp.float32)).reshape(flat_rows, groups, HD)
        grad_keys = key_factor * (grad_key_norm - key_norm * lax.optimization_barrier(jnp.mean(grad_key_norm * key_norm, axis=-1, keepdims=True)))
        grad_keys = grad_keys.astype(jnp.bfloat16).reshape(flat_rows, groups * HD)
        grad_values = jnp.einsum('bghtj,btghd->bjgd', weights.astype(jnp.float32), grad_rows)
        grad_values = grad_values.astype(jnp.bfloat16).reshape(flat_rows, groups * HD)
        dims = (((1,), (1,)), ((), ()))
        vision_grad = vision_grad + lax.dot_general(grad_keys, w_key[section], dims, preferred_element_type=jnp.float32)
        vision_grad = vision_grad + lax.dot_general(grad_values, w_value[section], dims, preferred_element_type=jnp.float32)

        def add_group(group_index, carry):
            first_row = (group_index * group_rows).astype(jnp.int32)
            block_vision = lax.dynamic_slice_in_dim(flat_vision, first_row, group_rows, 0)
            block_keys = lax.dynamic_slice_in_dim(grad_keys, first_row, group_rows, 0)
            block_values = lax.dynamic_slice_in_dim(grad_values, first_row, group_rows, 0)
            inner = (((0,), (0,)), ((), ()))
            key_term = lax.dot_general(block_vision, block_keys, inner, preferred_element_type=jnp.float32).astype(jnp.bfloat16)
            value_term = lax.dot_general(block_vision, block_values, inner, preferred_element_type=jnp.float32).astype(jnp.bfloat16)
            key_term = lax.optimization_barrier(key_term)
            value_term = lax.optimization_barrier(value_term)
            return (carry[0] + key_term.astype(jnp.float32), carry[1] + value_term.astype(jnp.float32))
        zeros_init = jnp.zeros((D, groups * HD), jnp.float32)
        key_total, value_total = lax.fori_loop(0, N_DP, add_group, (zeros_init, zeros_init))
        key_totals.append(key_total)
        value_totals.append(value_total)
    grad_vision = vision_grad.reshape(N_DP, group_rows, D)
    return (jnp.stack(contexts), grad_vision, jnp.stack(key_totals), jnp.stack(value_totals))
```

```python
import math

import jax
import jax.numpy as jnp
from jax import lax
from jax.sharding import PartitionSpec as P

EPSILON = 1e-06
F32 = jnp.float32
BF16 = jnp.bfloat16


def normalize(values_in):
    factor = lax.rsqrt(jnp.mean(values_in * values_in, axis=-1, keepdims=True) + EPSILON)
    return (values_in * factor, factor)


def partner(index, step, size):
    if size & (size - 1) == 0:
        return index ^ step
    return (index + step) % size


def source(index, step, size):
    if size & (size - 1) == 0:
        return index ^ step
    return (index - step) % size


def swap(value, axis, step, size):
    return lax.ppermute(value, axis, [(i, partner(i, step, size)) for i in range(size)])


def block_of(value, index, size, axis):
    return lax.dynamic_slice_in_dim(value, index * size, size, axis)


def build(mesh):
    n_seg, n_dp, n_mp = (mesh.shape[name] for name in ("segment", "dp", "mp"))

    def per_device(queries, vision, w_key, w_value, masks, lengths, grad_context):
        seg, dp, mp = (lax.axis_index(name) for name in ("segment", "dp", "mp"))
        samples, part, width = vision.shape
        tile_rows = part * n_seg
        rows = samples * tile_rows
        hd = w_key.shape[2]
        own = vision.reshape(samples * part, width)
        parts = [own] + [swap(own, "segment", r, n_seg) for r in range(1, n_seg)]
        columns = width // n_dp
        slices = [block_of(own, dp, columns, 1)]
        for k in range(1, n_dp):
            slices.append(swap(block_of(own, partner(dp, k, n_dp), columns, 1), "dp", k, n_dp))
        slices = jnp.concatenate(slices, axis=0)
        columns_of = [slices] + [swap(slices, "segment", r, n_seg) for r in range(1, n_seg)]

        weight_pair = jnp.concatenate([w_key[0], w_value[0]], axis=1)
        projected = jnp.zeros((samples, tile_rows, 2 * hd), F32)
        for r, piece in enumerate(parts):
            product = jnp.dot(piece, weight_pair, preferred_element_type=F32)
            projected = lax.dynamic_update_slice_in_dim(
                projected, product.reshape(samples, part, 2 * hd), source(seg, r, n_seg) * part, 1
            )
        projected = projected.reshape(rows, 2 * hd)
        key_norm, key_factor = normalize(projected[:, :hd])
        key_rows = key_norm.astype(BF16).reshape(samples, tile_rows, hd)
        value_rows = projected[:, hd:].astype(BF16).reshape(samples, tile_rows, hd)
        head_count = queries.shape[3] // hd
        text_rows = queries.shape[2]
        query_raw = queries[0].astype(F32).reshape(samples, text_rows, head_count, hd)
        query_rows = normalize(query_raw)[0].astype(BF16)
        spread = jnp.broadcast_to(
            masks[:, :, None, :, None],
            (
                samples,
                masks.shape[1],
                text_rows // masks.shape[1],
                masks.shape[2],
                tile_rows // masks.shape[2],
            ),
        ).reshape(samples, text_rows, tile_rows)
        position = jnp.arange(text_rows, dtype=jnp.int32)
        allowed = jnp.where(
            (spread == 1) & (position[None, :, None] < lengths[:, None, None]), 1.0, 0.0
        ).astype(F32)
        root_scale = 1.0 / math.sqrt(hd)
        scores = (
            jnp.einsum("bthd,bjd->bhtj", query_rows, key_rows, preferred_element_type=F32)
            * root_scale
        )
        exponent = jnp.exp(scores) * allowed[:, None]
        denominator = jnp.sum(exponent, axis=-1, keepdims=True)
        probability = exponent / jnp.where(denominator > 0, denominator, 1.0)
        weights = probability.astype(BF16)
        context = jnp.einsum("bhtj,bjd->bthd", weights, value_rows, preferred_element_type=F32)
        context = context.astype(BF16).reshape(1, samples, text_rows, head_count * hd)
        grad_rows = grad_context[0].reshape(samples, text_rows, head_count, hd)
        grad_weights = jnp.einsum("bthd,bjd->bhtj", grad_rows, value_rows, preferred_element_type=F32)
        grad_scores = (
            probability
            * (grad_weights - jnp.sum(probability * grad_weights, axis=-1, keepdims=True))
            * root_scale
        ).astype(BF16)
        grad_key_norm = jnp.einsum(
            "bhtj,bthd->bjd", grad_scores, query_rows, preferred_element_type=F32
        ).reshape(rows, hd)
        grad_keys = key_factor * (
            grad_key_norm - key_norm * jnp.mean(grad_key_norm * key_norm, axis=-1, keepdims=True)
        )
        grad_values = jnp.einsum(
            "bhtj,bthd->bjd", weights, grad_rows, preferred_element_type=F32
        ).reshape(rows, hd)
        pair_grads = jnp.concatenate([grad_keys.astype(BF16), grad_values.astype(BF16)], axis=1)

        def vision_rows(segment):
            return lax.dot_general(
                block_of(pair_grads, segment, rows // n_seg, 0),
                weight_pair,
                (((1,), (1,)), ((), ())),
                preferred_element_type=F32,
            )

        away = [
            swap(vision_rows(partner(seg, r, n_seg)).astype(BF16), "segment", r, n_seg)
            for r in range(1, n_seg)
        ]
        total = vision_rows(seg)
        for piece in away:
            total = total + piece.astype(F32)
        out_rows = rows // (n_seg * n_mp)
        fold = 16 // math.gcd(out_rows, 16)
        folded = total.astype(BF16).reshape(n_mp, out_rows * fold, width // fold)
        kept = lax.dynamic_index_in_dim(total.reshape(n_mp, out_rows, width), mp, 0, keepdims=False)
        for k in reversed(range(1, n_mp)):
            sent = lax.dynamic_index_in_dim(folded, partner(mp, k, n_mp), 0, keepdims=False)
            kept = kept + swap(sent, "mp", k, n_mp).astype(F32).reshape(out_rows, width)
        grad_vision = kept.reshape(1, out_rows, width)

        by_part = pair_grads.reshape(samples, n_seg, part, 2 * hd)
        ordered = jnp.stack(
            [
                lax.dynamic_index_in_dim(by_part, source(seg, r, n_seg), 1, keepdims=False)
                for r in range(n_seg)
            ]
        ).reshape(n_seg, samples * part, 2 * hd)
        groups = jnp.stack(
            [ordered] + [swap(ordered, "dp", k, n_dp) for k in range(1, n_dp)], axis=1
        )
        grad_w = lax.dot_general(
            jnp.concatenate(columns_of, axis=0),
            groups.reshape(n_seg * n_dp * samples * part, 2 * hd),
            (((0,), (0,)), ((), ())),
            preferred_element_type=F32,
        )
        return (context, grad_vision, grad_w[None, :, :hd], grad_w[None, :, hd:])

    return per_device


def solution(mesh):
    in_specs = (
        P("segment", "dp", None, "mp"),
        P("dp", "segment", None),
        P("segment", None, "mp"),
        P("segment", None, "mp"),
        P("dp", None, None),
        P("dp"),
        P("segment", "dp", None, "mp"),
    )
    out_specs = (
        P("segment", "dp", None, "mp"),
        P("dp", ("segment", "mp"), None),
        P("segment", "dp", "mp"),
        P("segment", "dp", "mp"),
    )
    return jax.shard_map(
        build(mesh), mesh=mesh, in_specs=in_specs, out_specs=out_specs, check_vma=False
    )
```

```python
import functools
import math

import jax
import jax.numpy as jnp
from jax import lax
from jax.experimental import pallas as pl
from jax.experimental.pallas import tpu as pltpu
from jax.sharding import PartitionSpec as P

EPSILON = 1e-06
KERNEL_BYTES = 16 << 20
F32 = jnp.float32
BF16 = jnp.bfloat16
VMEM = pl.BlockSpec(memory_space=pltpu.VMEM)
SMEM = pl.BlockSpec(memory_space=pltpu.SMEM)
NT = (((1,), (1,)), ((), ()))
TN = (((0,), (0,)), ((), ()))


def partner(index, step, size):
    if size & (size - 1) == 0:
        return index ^ step
    return (index + step) % size


def source(index, step, size):
    if size & (size - 1) == 0:
        return index ^ step
    return (index - step) % size


def swap(value, axis, step, size):
    return lax.ppermute(value, axis, [(i, partner(i, step, size)) for i in range(size)])


def cost(flops, moved, transcendentals=0):
    return pl.CostEstimate(flops=flops, bytes_accessed=moved, transcendentals=transcendentals)


def chunk_of(length, largest):
    best = length
    for size in range(128, largest + 1, 128):
        if length % size == 0:
            best = size
    return min(best, length)


def params():
    return pltpu.CompilerParams(vmem_limit_bytes=KERNEL_BYTES)


def norm_kernel(hd, q_ref, qn_ref):

    for m in range(q_ref.shape[1]):
        for h in range(q_ref.shape[3] // hd):
            lanes = slice(h * hd, (h + 1) * hd)
            x = q_ref[0, m, :, lanes].astype(F32)
            factor = lax.rsqrt(jnp.mean(x * x, axis=-1, keepdims=True) + EPSILON)
            qn_ref[m, :, lanes] = (x * factor).astype(BF16)


def norm_call(queries, hd):
    return pl.pallas_call(
        functools.partial(norm_kernel, hd),
        in_specs=[VMEM],
        out_specs=VMEM,
        out_shape=jax.ShapeDtypeStruct(queries.shape[1:], BF16),
        cost_estimate=cost(4 * queries.size, 4 * queries.size),
        compiler_params=params(),
        name="norm",
    )(queries)


def packed_rows(rows, columns, width):
    return 16 * -(-(rows // 16) // (columns // width))


def packed_block(t, columns, width):
    side = columns // width
    return slice(t // side * 16, t // side * 16 + 16), slice(t % side * width, (t % side + 1) * width)


def spread(lhs, wk_ref, wv_ref, folds, begin, step):
    columns = wk_ref.shape[0] // folds
    total = None
    for f in range(folds):
        rows = pl.ds(f * columns + begin, step)
        pair = jnp.concatenate([wk_ref[rows, :], wv_ref[rows, :]], axis=1)
        term = lax.dot_general(lhs(f), pair, NT, preferred_element_type=F32)
        total = term if total is None else total + term
    return total


def attend_kernel(sizes, place_ref, masks_ref, lengths_ref, wk_ref, wv_ref, qn_ref, gc_ref, *refs):
    n_seg, n_dp, n_mp, folds, out_rows = sizes
    part_refs, refs = refs[:n_seg], refs[n_seg:]
    grads_ref, weights_ref, values_ref, lhs_ref = refs[:4]
    away_refs, refs = refs[4 : 3 + n_seg], refs[3 + n_seg :]
    message_refs, (proj_ref, order_ref, scratch_ref) = refs[: n_dp - 1], refs[n_dp - 1 :]
    held, width = part_refs[0].shape
    hd = wk_ref.shape[1]
    samples, text = qn_ref.shape[:2]
    part = held // samples
    tokens = part * n_seg
    rows = tokens * samples
    heads = qn_ref.shape[2] // hd
    blocks, tiles = masks_ref.shape[1], masks_ref.shape[2]
    root_scale = 1.0 / math.sqrt(hd)
    seg, dp, mp = place_ref[0], place_ref[1], place_ref[2]

    step = chunk_of(width, 2048)
    total = None
    for begin in range(0, width, step):
        chunk = slice(begin, begin + step)
        lhs = jnp.concatenate([ref[:, chunk] for ref in part_refs], axis=0)
        pair = jnp.concatenate([wk_ref[chunk, :], wv_ref[chunk, :]], axis=1)
        term = jnp.dot(lhs, pair, preferred_element_type=F32)
        total = term if total is None else total + term
    proj_ref[...] = total

    row = lax.broadcasted_iota(jnp.int32, (tokens, text), 0)
    position = lax.broadcasted_iota(jnp.int32, (tokens, text), 1)
    token = jnp.zeros((tokens, text), jnp.int32)
    for r in range(n_seg):
        moved = row - r * part + source(seg, r, n_seg) * part
        token = jnp.where(row // part == r, moved, token)
    for m in range(samples):
        raw = jnp.concatenate(
            [proj_ref[r * held + m * part : r * held + (m + 1) * part, :] for r in range(n_seg)], axis=0
        )
        key_raw = raw[:, :hd]
        key_factor = lax.rsqrt(jnp.mean(key_raw * key_raw, axis=-1, keepdims=True) + EPSILON)
        key_norm = key_raw * key_factor
        keys = key_norm.astype(BF16)
        values = raw[:, hd:].astype(BF16)
        values_ref[m] = values
        allowed = jnp.zeros((tokens, text), F32)
        for block in range(blocks):
            for tile in range(tiles):
                inside = (token // (tokens // tiles) == tile) & (position // (text // blocks) == block)
                allowed = jnp.where(inside & (masks_ref[m, block, tile] == 1), 1.0, allowed)
        allowed = jnp.where(position < lengths_ref[m], allowed, 0.0)
        grad_key_norm = jnp.zeros((tokens, hd), F32)
        grad_values = jnp.zeros((tokens, hd), F32)
        for h in range(heads):
            lanes = slice(h * hd, (h + 1) * hd)
            query = qn_ref[m, :, lanes]
            grads = gc_ref[0, m, :, lanes]
            scores = lax.dot_general(keys, query, NT, preferred_element_type=F32) * root_scale
            exponent = jnp.exp(scores) * allowed
            total = jnp.sum(exponent, axis=0, keepdims=True)
            probability = exponent * (1.0 / jnp.where(total > 0, total, 1.0))
            weights = probability.astype(BF16)
            weights_ref[m, h] = weights
            grad_weights = lax.dot_general(values, grads, NT, preferred_element_type=F32)
            inner = jnp.sum(probability * grad_weights, axis=0, keepdims=True)
            grad_scores = (probability * (grad_weights - inner) * root_scale).astype(BF16)
            grad_key_norm += jnp.dot(grad_scores, query, preferred_element_type=F32)
            grad_values += jnp.dot(weights, grads, preferred_element_type=F32)
        inner = jnp.mean(grad_key_norm * key_norm, axis=-1, keepdims=True)
        grad_keys = key_factor * (grad_key_norm - key_norm * inner)
        for r in range(n_seg):
            here = slice(r * held + m * part, r * held + (m + 1) * part)
            there = slice(r * part, (r + 1) * part)
            order_ref[here, :hd] = grad_keys[there]
            order_ref[here, hd:] = grad_values[there]
    ordered = order_ref[...].astype(BF16)
    grads_ref[...] = ordered

    size = folds * out_rows
    count = n_mp * size
    row = lax.broadcasted_iota(jnp.int32, (count, rows), 0)
    column = lax.broadcasted_iota(jnp.int32, (count, rows), 1)
    peer = row // size
    fold = (row - peer * size) // out_rows
    index = row - peer * size - fold * out_rows
    for r in range(n_seg):
        wanted = partner(seg, r, n_seg) * (rows // n_seg) + partner(mp, peer, n_mp) * out_rows + index
        sample = wanted // tokens
        place = wanted - sample * tokens
        owner = place // part
        wanted = source(seg, owner, n_seg) * held + sample * part + place - owner * part
        target = lhs_ref if r == 0 else scratch_ref
        for f in range(folds):
            chosen = jnp.where((column == wanted) & (fold == f), 1.0, 0.0).astype(BF16)
            target[f] = jnp.dot(chosen, ordered, preferred_element_type=F32).astype(BF16)
        if r > 0:
            columns = width // folds
            step = chunk_of(columns, 1024)
            for begin in range(0, columns, step):
                away_refs[r - 1][:, begin : begin + step] = spread(
                    lambda f: scratch_ref[f], wk_ref, wv_ref, folds, begin, step
                ).astype(BF16)

    columns = width // n_dp
    top = packed_rows(rows, columns, 2 * hd)
    for k, message_ref in enumerate(message_refs, 1):
        begin = pl.multiple_of(partner(dp, k, n_dp) * columns, 128)
        message_ref[top:, :] = part_refs[0][:, pl.ds(begin, columns)]
        for t in range(rows // 16):
            down, along = packed_block(t, columns, 2 * hd)
            message_ref[down, along] = ordered[t * 16 : (t + 1) * 16]


def attend_call(sizes, place, masks, lengths, wk, wv, qn, gc, parts):
    n_seg, n_dp, n_mp, folds, out_rows = sizes
    held, width = parts[0].shape
    hd = wk.shape[1]
    samples, text = qn.shape[:2]
    heads = qn.shape[2] // hd
    tokens = held // samples * n_seg
    rows = held * n_seg
    count = n_mp * folds * out_rows
    columns = width // n_dp
    top = packed_rows(rows, columns, 2 * hd)
    shape = jax.ShapeDtypeStruct
    return pl.pallas_call(
        functools.partial(attend_kernel, sizes),
        in_specs=[SMEM] * 3 + [VMEM] * (4 + n_seg),
        out_specs=[VMEM] * (3 + n_seg + n_dp - 1),
        out_shape=[
            shape((rows, 2 * hd), BF16),
            shape((samples, heads, tokens, text), BF16),
            shape((samples, tokens, hd), BF16),
            shape((folds, count, 2 * hd), BF16),
        ]
        + [shape((count, width // folds), BF16)] * (n_seg - 1)
        + [shape((top + held, columns), BF16)] * (n_dp - 1),
        scratch_shapes=[
            pltpu.VMEM((rows, 2 * hd), F32),
            pltpu.VMEM((rows, 2 * hd), F32),
            pltpu.VMEM((folds, count, 2 * hd), BF16),
        ],
        cost_estimate=cost(8 * rows * width * hd + 8 * qn.size * tokens, 4 * wk.size + 8 * qn.size),
        compiler_params=params(),
        name="attend",
    )(place, masks, lengths, wk, wv, qn, gc, *parts)


def context_kernel(weights_ref, values_ref, out_ref):
    samples, heads = weights_ref.shape[:2]
    hd = values_ref.shape[2]
    for m in range(samples):
        for h in range(heads):
            product = lax.dot_general(
                weights_ref[m, h], values_ref[m], TN, preferred_element_type=F32
            )
            out_ref[0, m, :, h * hd : (h + 1) * hd] = product.astype(BF16)


def context_call(weights, values):
    samples, heads, tokens, text = weights.shape
    hd = values.shape[2]
    return pl.pallas_call(
        context_kernel,
        in_specs=[VMEM, VMEM],
        out_specs=VMEM,
        out_shape=jax.ShapeDtypeStruct((1, samples, text, heads * hd), BF16),
        cost_estimate=cost(2 * weights.size * hd, 2 * weights.size + 2 * samples * text * heads * hd),
        compiler_params=params(),
        name="context",
    )(weights, values)


def spread_kernel(n_mp, added, lhs_ref, wk_ref, wv_ref, *refs):
    folds = lhs_ref.shape[0]
    added_refs, outs = refs[:added], refs[added:]
    columns = wk_ref.shape[0] // folds
    size = lhs_ref.shape[1] // n_mp
    step = chunk_of(columns, 1024)
    for begin in range(0, columns, step):
        chunk = slice(begin, begin + step)
        total = spread(lambda f: lhs_ref[f], wk_ref, wv_ref, folds, begin, step)
        for other in added_refs:
            total = total + other[:, chunk].astype(F32)
        for k, out in enumerate(outs):
            out[:, chunk] = total[k * size : (k + 1) * size].astype(out.dtype)


def spread_call(lhs, wk, wv, added, n_mp):
    folds, rows, depth = lhs.shape
    width, hd = wk.shape
    columns = width // folds
    return pl.pallas_call(
        functools.partial(spread_kernel, n_mp, len(added)),
        in_specs=[VMEM] * (3 + len(added)),
        out_specs=[VMEM] * n_mp,
        out_shape=[
            jax.ShapeDtypeStruct((rows // n_mp, columns), BF16 if k else F32) for k in range(n_mp)
        ],
        cost_estimate=cost(4 * rows * width * hd, 4 * wk.size + 2 * rows * columns),
        compiler_params=params(),
        name="spread",
    )(lhs, wk, wv, *added)


def finish_kernel(*refs):
    out_ref = refs[-1]
    total = refs[0][...]
    for ref in refs[1:-1]:
        total = total + ref[...].astype(F32)
    size, columns = out_ref.shape[1], total.shape[1]
    for f in range(total.shape[0] // size):
        out_ref[0, :, f * columns : (f + 1) * columns] = total[f * size : (f + 1) * size]


def finish_call(own, others, size):
    rows, columns = own.shape
    width = rows * columns // size
    return pl.pallas_call(
        finish_kernel,
        in_specs=[VMEM] * (1 + len(others)),
        out_specs=VMEM,
        out_shape=jax.ShapeDtypeStruct((1, size, width), F32),
        cost_estimate=cost(4 * own.size, 8 * own.size + 2 * own.size * len(others)),
        compiler_params=params(),
        name="finish",
    )(own, *others)


def weight_kernel(n_seg, n_dp, place_ref, grads_ref, *refs):
    part_refs, message_refs, (gk_ref, gv_ref) = refs[:n_seg], refs[n_seg:-2], refs[-2:]
    rows, width = grads_ref.shape
    hd = width // 2
    held = part_refs[0].shape[0]
    columns = gk_ref.shape[1]
    top = packed_rows(rows, columns, width)
    dp = place_ref[1]
    per = n_dp - 1
    grads = [grads_ref[...]]
    for ref in message_refs[:per]:
        blocks = [packed_block(t, columns, width) for t in range(rows // 16)]
        grads.append(jnp.concatenate([ref[down, along] for down, along in blocks], axis=0))
    stacked = jnp.concatenate(
        [grads[k][r * held : (r + 1) * held] for r in range(n_seg) for k in range(n_dp)], axis=0
    )
    step = chunk_of(columns, 512)
    for begin in range(0, columns, step):
        tokens = []
        for r in range(n_seg):
            first = pl.multiple_of(dp * columns + begin, 128)
            tokens.append(part_refs[r][:, pl.ds(first, step)])
            for k in range(per):
                tokens.append(message_refs[r * per + k][top:, begin : begin + step])
        product = lax.dot_general(
            jnp.concatenate(tokens, axis=0), stacked, TN, preferred_element_type=F32
        )
        gk_ref[0, begin : begin + step, :] = product[:, :hd]
        gv_ref[0, begin : begin + step, :] = product[:, hd:]


def weight_call(n_seg, n_dp, place, grads, parts, messages):
    rows, width = grads.shape
    columns = parts[0].shape[1] // n_dp
    hd = width // 2
    return pl.pallas_call(
        functools.partial(weight_kernel, n_seg, n_dp),
        in_specs=[SMEM] + [VMEM] * (1 + len(parts) + len(messages)),
        out_specs=[VMEM] * 2,
        out_shape=[jax.ShapeDtypeStruct((1, columns, hd), F32)] * 2,
        cost_estimate=cost(
            2 * n_dp * rows * columns * width, 2 * n_dp * rows * columns + 8 * columns * hd
        ),
        compiler_params=params(),
        name="weight",
    )(place, grads, *parts, *messages)


def build(mesh):
    n_seg, n_dp, n_mp = (mesh.shape[name] for name in ("segment", "dp", "mp"))

    def per_device(queries, vision, w_key, w_value, masks, lengths, grad_context):
        samples, part, width = vision.shape
        rows = samples * part * n_seg
        wk, wv = w_key[0], w_value[0]
        out_rows = rows // (n_seg * n_mp)
        folds = 8 // math.gcd(out_rows, 8)
        sizes = (n_seg, n_dp, n_mp, folds, out_rows)
        place = jnp.stack([lax.axis_index(name) for name in ("segment", "dp", "mp")]).astype(jnp.int32)
        own = vision.reshape(samples * part, width)
        parts = [own] + [swap(own, "segment", r, n_seg) for r in range(1, n_seg)]
        qn = norm_call(queries, wk.shape[1])
        outs = attend_call(sizes, place, masks, lengths, wk, wv, qn, grad_context, parts)
        grads, weights, values, lhs = outs[:4]
        away = [swap(outs[3 + r], "segment", r, n_seg) for r in range(1, n_seg)]
        messages = outs[3 + n_seg :]
        messages = [swap(messages[k - 1], "dp", k, n_dp) for k in range(1, n_dp)]
        totals = spread_call(lhs, wk, wv, away, n_mp)
        arrived = [swap(totals[k], "mp", k, n_mp) for k in reversed(range(1, n_mp))]
        context = context_call(weights, values)
        crossed = [swap(piece, "segment", r, n_seg) for r in range(1, n_seg) for piece in messages]
        grad_wk, grad_wv = weight_call(n_seg, n_dp, place, grads, parts, messages + crossed)
        grad_vision = finish_call(totals[0], arrived, out_rows)
        return (context, grad_vision, grad_wk, grad_wv)

    return per_device


def solution(mesh):
    in_specs = (
        P("segment", "dp", None, "mp"),
        P("dp", "segment", None),
        P("segment", None, "mp"),
        P("segment", None, "mp"),
        P("dp", None, None),
        P("dp"),
        P("segment", "dp", None, "mp"),
    )
    out_specs = (
        P("segment", "dp", None, "mp"),
        P("dp", ("segment", "mp"), None),
        P("segment", "dp", "mp"),
        P("segment", "dp", "mp"),
    )
    return jax.shard_map(
        build(mesh), mesh=mesh, in_specs=in_specs, out_specs=out_specs, check_vma=False
    )
```
